32 devices in a mesh: snap: 2 (over core), brick: 16 (over z, y, x).
Axes of the slice: x: 2, y: 2, z: 4, core: 2. Of those that a mesh axis runs over, the one named last changes fastest.
Arguments:
- atom_features: bfloat16 [2, 32, 262144], P('snap', None, 'brick'), may hold values from -6 to 6
- cotangent: bfloat16 [2, 32, 262144], P('snap', None, 'brick'), may hold values from -6 to 6
- cell_index: int32 [2, 4, 262144], P('snap', None, 'brick'), may hold values from 0 to 39, as said below
- assign_weight: float32 [2, 4, 262144], P('snap', None, 'brick'), may hold values from 0.05 to 1
- conv_kernel: bfloat16 [27, 32, 32], replicated, may hold values from -0.21875 to 0.21875
- spectral_gain: float32 [32, 128, 128], P(None, None, 'brick'), may hold values from 0.1 to 2
Outputs:
- atom_grad: bfloat16 [2, 32, 262144], P('snap', None, 'brick')
- kernel_grad: float32 [27, 32, 32], replicated
- gain_grad: float32 [32, 128, 128], P(None, None, 'brick')
The draws below stay inside these ranges and needn't reach their ends.
Inputs may be any that keep to these rules, and one draw needn't show every extreme that they name: `cell_index`: for each slot there are p from 0 to 8 and z from 0 to 2 such that its four corners are, in order, p * 4 + z, (p + 1) * 4 + z, p * 4 + z + 1 and (p + 1) * 4 + z + 1.
All inputs are finite; a program needn't handle non-finite values.
Results may differ from the reference program's by a relative error of at most 0.0058.
Values may be sent and summed in bfloat16 or wider, within the bound.
A program may use at most 64 MiB of HBM per device.

```python
import math
import jax
import jax.numpy as jnp
from jax import lax

C = 32
NX = 128
NY = 128
NZ = 4
SLOTS = 128
CORNERS = 4
SNAPS = 2
XDEV = 8
ATOM_DEV = 16384
ATOMS = 262144


def draw_cell_index(key, part):
    first_key, second_key = jax.random.split(jax.random.fold_in(key, 17))
    plane_base = jax.random.randint(first_key, (SNAPS, ATOMS), 0, XDEV + 1)
    depth_base = jax.random.randint(second_key, (SNAPS, ATOMS), 0, NZ - 1)
    corners = [plane_base * NZ + depth_base, (plane_base + 1) * NZ + depth_base, plane_base * NZ + depth_base + 1, (plane_base + 1) * NZ + depth_base + 1]
    return jnp.stack(corners, axis=1).astype(jnp.int32)


def level_of(rng, extent, shards, smallest, largest):
    def one(position, shards_of):
        heights = jax.random.uniform(jax.random.fold_in(jax.random.fold_in(rng, 6), position), (shards_of,), jnp.float32, smallest / len(shards), largest / len(shards))
        return jnp.repeat(jnp.exp(heights), extent[position] // shards_of).reshape((-1,) + (1,) * (len(extent) - position - 1))

    level = one(*shards[0])
    for cut in shards[1:]:
        level = level * one(*cut)
    return level


def normal_values(rng, dims, deviation, limit, cuts=(), kind=jnp.bfloat16):
    level = level_of(rng, dims, cuts, -0.22, 0.18) if cuts else 1.0
    drawn = jax.random.normal(rng, dims, jnp.float32) * deviation * level
    return jnp.minimum(jnp.maximum(drawn, -limit), limit).astype(kind)


def setup_inputs(seed: int = 0) -> dict:
    streams_of = jax.random.split(jax.random.key(seed), 7)
    atom_features = normal_values(streams_of[0], (SNAPS, C, ATOMS), 1.0, 6.0, ((0, 2), (2, 16)))
    cotangent = normal_values(streams_of[1], (SNAPS, C, ATOMS), 1.0, 6.0, ((0, 2), (2, 16)))
    cell_index = draw_cell_index(jax.random.fold_in(streams_of[6], 71), 0)
    assign_weight = jnp.clip(0.05 + 0.95 * jax.random.uniform(streams_of[3], (SNAPS, CORNERS, ATOMS), jnp.float32) ** level_of(streams_of[3], (SNAPS, CORNERS, ATOMS), ((0, 2), (2, 16)), -0.2, 0.2), 0.05, 1.0)
    conv_kernel = normal_values(streams_of[4], (27, C, C), (27 * C) ** -0.5, 0.21875)
    spectral_gain = jnp.clip(0.1 + 1.9 * jax.random.uniform(streams_of[5], (C, NX, NY), jnp.float32) ** level_of(streams_of[5], (C, NX, NY), ((2, 16),), -0.2, 0.2), 0.1, 2.0)
    return {"atom_features": atom_features, "cotangent": cotangent, "cell_index": cell_index, "assign_weight": assign_weight, "conv_kernel": conv_kernel, "spectral_gain": spectral_gain}


def offset_list():
    return [(first, second, third) for first in (-1, 0, 1) for second in (-1, 0, 1) for third in (-1, 0, 1)]

def displaced(volume, offsets):
    moved = jnp.roll(volume, (-offsets[0], -offsets[1]), axis=(1, 2))
    if offsets[2] == 1:
        moved = jnp.concatenate([moved[..., 1:], jnp.zeros_like(moved[..., :1])], axis=-1)
    elif offsets[2] == -1:
        moved = jnp.concatenate([jnp.zeros_like(moved[..., :1]), moved[..., :-1]], axis=-1)
    return moved

def rounded(values):
    return lax.optimization_barrier(values.astype(jnp.bfloat16)).astype(jnp.float32)

def reference(atom_features, cotangent, cell_index, assign_weight, conv_kernel, spectral_gain):
    atom_ids = jnp.arange(ATOMS, dtype=jnp.int32)
    brick_of = atom_ids // ATOM_DEV
    row_of = atom_ids % ATOM_DEV // SLOTS
    kernel_f = conv_kernel.astype(jnp.float32)
    offsets_all = offset_list()
    kernel_total = jnp.zeros((27, C, C), jnp.float32)
    gain_total = jnp.zeros((C, NX, NY), jnp.float32)
    results = []
    for snap_id in range(SNAPS):
        weight_bf = rounded(assign_weight[snap_id])
        plane_local = cell_index[snap_id] // NZ
        depth_local = cell_index[snap_id] % NZ
        plane_global = (brick_of[None, :] * XDEV + plane_local - 1) % NX
        flat_cell = ((plane_global * NY + row_of[None, :]) * NZ + depth_local).astype(jnp.int32)
        features = jnp.concatenate([atom_features[snap_id].astype(jnp.float32), cotangent[snap_id].astype(jnp.float32)], axis=0)
        spread = jnp.zeros((2 * C, NX * NY * NZ), jnp.float32)
        for corner in range(CORNERS):
            spread = spread.at[:, flat_cell[corner]].add(weight_bf[corner][None, :] * features)
        spread = spread.reshape(2 * C, NX, NY, NZ)
        state = rounded(spread[:C])
        grad_mesh = spread[C:]
        mixed = state
        for tap, offsets in enumerate(offsets_all):
            mixed = mixed + jnp.einsum('cxyz,cd->dxyz', displaced(state, offsets), kernel_f[tap])
        grad_freq = jnp.fft.fft2(grad_mesh, axes=(1, 2))
        mixed_freq = jnp.fft.fft2(mixed, axes=(1, 2))
        gain_total = gain_total + lax.optimization_barrier(jnp.sum(jnp.real(jnp.conj(grad_freq) * mixed_freq), axis=3))
        grad_mixed = jnp.real(jnp.fft.ifft2(spectral_gain[..., None] * grad_freq, axes=(1, 2)))
        grad_state = rounded(grad_mixed)
        pulled_sum = grad_state
        tap_grads = []
        for tap, offsets in enumerate(offsets_all):
            negated = (-offsets[0], -offsets[1], -offsets[2])
            pulled_sum = pulled_sum + jnp.einsum('dxyz,cd->cxyz', displaced(grad_state, negated), kernel_f[tap])
            tap_grads.append(jnp.einsum('cxyz,dxyz->cd', displaced(state, offsets), grad_state))
        kernel_total = kernel_total + jnp.stack(tap_grads)
        pulled = rounded(pulled_sum).reshape(C, NX * NY * NZ)
        atom_total = jnp.zeros((C, ATOMS), jnp.float32)
        for corner in range(CORNERS):
            atom_total = atom_total + weight_bf[corner][None, :] * pulled[:, flat_cell[corner]]
        results.append(atom_total.astype(jnp.bfloat16))
    kernel_grad = kernel_total / math.sqrt(SNAPS * NX * NY * NZ)
    gain_grad = gain_total / (NX * NY * math.sqrt(SNAPS * NZ))
    return (jnp.stack(results), kernel_grad, gain_grad)
```

```python
import math

import jax
import jax.numpy as jnp
from jax import lax
import numpy as np
from jax.experimental import pallas as pl
from jax.experimental.pallas import tpu as pltpu
from jax.sharding import PartitionSpec as P

NX = 128
NY = 128
NZ = 4
CORNERS = 4


HIGHEST = lax.Precision.HIGHEST


def from_behind(value, axis, steps):
    count = lax.axis_size(axis)
    pairs = [(source, (source + steps) % count) for source in range(count)]
    return lax.ppermute(value, axis, pairs)


def with_halo(cells, sides, width):
    for axis, dim in sides:
        count = lax.axis_size(axis)
        head = lax.slice_in_dim(cells, 0, width, axis=dim)
        tail = lax.slice_in_dim(cells, cells.shape[dim] - width, cells.shape[dim], axis=dim)
        cells = jnp.concatenate(
            [
                lax.ppermute(tail, axis, [(i, (i + 1) % count) for i in range(count)]),
                cells,
                lax.ppermute(head, axis, [((i + 1) % count, i) for i in range(count)]),
            ],
            axis=dim,
        )
    return cells


def tables(length):
    indices = jnp.arange(length, dtype=jnp.int32)
    phases = indices[:, None] * indices[None, :] % length
    angles = phases.astype(jnp.float32) * (2.0 * math.pi / length)
    return (jnp.cos(angles), jnp.sin(angles))


def patches(padded, first_plane, planes):
    row_total = padded.shape[1]
    thickness = padded.shape[3]
    wrapped = jnp.concatenate([padded[:, -1:], padded, padded[:, :1]], axis=1)
    widened = jnp.pad(wrapped, ((0, 0), (0, 0), (0, 0), (1, 1)))
    pieces = []
    for step_first in (-1, 0, 1):
        for step_second in (-1, 0, 1):
            for step_third in (-1, 0, 1):
                pieces.append(
                    widened[
                        :,
                        1 + step_second : 1 + step_second + row_total,
                        first_plane + step_first : first_plane + step_first + planes,
                        1 + step_third : 1 + step_third + thickness,
                    ]
                )
    return jnp.stack(pieces)


def transform_rows(mesh_field, row_cosine, row_sine):
    real_part = jnp.einsum("cyxz,yk->ckxz", mesh_field, row_cosine, precision=HIGHEST)
    imag_part = -jnp.einsum("cyxz,yk->ckxz", mesh_field, row_sine, precision=HIGHEST)
    return jnp.stack([real_part, imag_part])


def transform_columns(stacked, col_cosine, col_sine, sign_value):

    def apply_table(part_values, table):
        return jnp.einsum("ckxz,xq->ckqz", part_values, table, precision=HIGHEST)

    real_part = stacked[0]
    imag_part = stacked[1]
    new_real = apply_table(real_part, col_cosine) + sign_value * apply_table(imag_part, col_sine)
    new_imag = apply_table(imag_part, col_cosine) - sign_value * apply_table(real_part, col_sine)
    return jnp.stack([new_real, new_imag])


def shards(atom_features, cotangent, cell_index, assign_weight, conv_kernel, spectral_gain):
    channels = atom_features.shape[1]
    slot_count = atom_features.shape[2] // NY
    own_planes = NX // lax.axis_size("brick")
    tile_cells = (own_planes + 2) * NZ
    snap_count = lax.axis_size("snap")
    index_tiles = cell_index[0].reshape(CORNERS, NY, slot_count)
    weight_tiles = assign_weight[0].astype(jnp.bfloat16).reshape(CORNERS, NY, slot_count)
    cell_numbers = jnp.arange(tile_cells, dtype=jnp.int32)
    blocks = jnp.zeros((NY, tile_cells, slot_count), jnp.bfloat16)
    for corner in range(CORNERS):
        matches = index_tiles[corner][:, None, :] == cell_numbers[None, :, None]
        blocks = blocks + jnp.where(
            matches, weight_tiles[corner][:, None, :], jnp.zeros((), jnp.bfloat16)
        )
    stacked = jnp.concatenate([atom_features[0], cotangent[0]], axis=0).reshape(
        2 * channels, NY, slot_count
    )
    spread = jnp.einsum("cts,tjs->ctj", stacked, blocks, preferred_element_type=jnp.float32)
    spread = spread.reshape(2 * channels, NY, own_planes + 2, NZ)
    from_above = from_behind(spread[:, :, 0], "brick", -1)
    from_below = from_behind(spread[:, :, own_planes + 1], "brick", 1)
    owned_planes = spread[:, :, 1 : own_planes + 1]
    owned_planes = owned_planes.at[:, :, 0].add(from_below)
    owned_planes = owned_planes.at[:, :, own_planes - 1].add(from_above)
    state_bf = owned_planes[:channels].astype(jnp.bfloat16)
    grad_mesh = owned_planes[channels:]
    col_cosine, col_sine = tables(NX)
    row_cosine, row_sine = tables(NY)

    def make_rows(mesh_field):
        return transform_rows(mesh_field, row_cosine, row_sine)

    def to_columns(part_rows):
        return transform_columns(part_rows, col_cosine, col_sine, 1.0)

    grad_rows = make_rows(grad_mesh)
    grad_spec = to_columns(
        lax.all_to_all(grad_rows, "brick", split_axis=2, concat_axis=3, tiled=True)
    )
    state_rim = with_halo(state_bf, (("brick", 2),), 1)
    state_patch = patches(state_rim, 1, own_planes)
    conv_out = jnp.einsum(
        "tcyxz,tcd->dyxz", state_patch, conv_kernel, preferred_element_type=jnp.float32
    )
    mesh_mixed = state_bf.astype(jnp.float32) + conv_out
    mixed_rows = make_rows(mesh_mixed)
    state_spec = to_columns(
        lax.all_to_all(
            mixed_rows.astype(jnp.bfloat16), "brick", split_axis=2, concat_axis=3, tiled=True
        ).astype(mixed_rows.dtype)
    )
    products = jnp.sum(grad_spec[0] * state_spec[0] + grad_spec[1] * state_spec[1], axis=3)
    gain_part = jnp.transpose(products, (0, 2, 1)) / (NX * NY * math.sqrt(snap_count * NZ))
    gain_local = jnp.transpose(spectral_gain, (0, 2, 1))
    filtered = grad_spec * gain_local[None, :, :, :, None]
    before_cross = transform_columns(filtered, col_cosine, col_sine, -1.0)
    part_cols = lax.all_to_all(before_cross, "brick", split_axis=3, concat_axis=2, tiled=True)
    real_rows = jnp.einsum("ckxz,ky->cyxz", part_cols[0], row_cosine, precision=HIGHEST)
    imag_rows = jnp.einsum("ckxz,ky->cyxz", part_cols[1], row_sine, precision=HIGHEST)
    grad_mixed = (real_rows - imag_rows) / (NX * NY)
    grad_bf = grad_mixed.astype(jnp.bfloat16)
    flipped = conv_kernel[::-1]
    grad_padded = with_halo(grad_bf, (("brick", 2),), 1)
    grad_patch = patches(grad_padded, 1, own_planes)
    back_conv = jnp.einsum(
        "tdyxz,tcd->cyxz", grad_patch, flipped, preferred_element_type=jnp.float32
    )
    pulled = (grad_bf.astype(jnp.float32) + back_conv).astype(jnp.bfloat16)
    pulled_full = with_halo(pulled, (("brick", 2),), 1)
    kernel_part = jnp.einsum(
        "tcyxz,dyxz->tcd", state_patch, grad_bf, preferred_element_type=jnp.float32
    )
    kernel_part = kernel_part / math.sqrt(snap_count * NX * NY * NZ)
    pulled_tiles = pulled_full.reshape(channels, NY, tile_cells)
    atom_total = jnp.einsum(
        "ctj,tjs->cts", pulled_tiles, blocks, preferred_element_type=jnp.float32
    )
    atom_grad = atom_total.astype(jnp.bfloat16).reshape(1, channels, NY * slot_count)
    kernel_grad = lax.psum(kernel_part, ("snap", "brick"))
    gain_grad = lax.psum(gain_part, "snap")
    return (atom_grad, kernel_grad, gain_grad)


BF = jnp.bfloat16
F32 = jnp.float32
LANES = 128
ROWS = 8
PADX = 16
MESH = pl.DeviceIdType.MESH


def contract(left, right, dims, precision=None):
    return lax.dot_general(
        left, right, ((dims[:1], dims[1:]), ((), ())),
        precision=precision, preferred_element_type=F32,
    )


def vmem():
    return pl.BlockSpec(memory_space=pltpu.VMEM)


def local_call(body, out_shape, count, scratch=(), flops=0):
    return pl.pallas_call(
        body,
        out_shape=out_shape,
        in_specs=[vmem()] * count,
        out_specs=jax.tree.map(lambda _: vmem(), out_shape),
        scratch_shapes=list(scratch),
        compiler_params=pltpu.CompilerParams(vmem_limit_bytes=60 * 1024 * 1024),
    )


def shape_of(dims, kind):
    return jax.ShapeDtypeStruct(dims, kind)


def corner_block(index_ref, weight_ref, lanes, cell_of_row):
    block = jnp.zeros(cell_of_row.shape, F32)
    index = index_ref[:, lanes]
    weight = weight_ref[:, lanes]
    for corner in range(CORNERS):
        block = jnp.where(
            index[corner : corner + 1] == cell_of_row, weight[corner : corner + 1], block
        )
    return block.astype(BF)


def row_cells():
    row = lax.broadcasted_iota(jnp.int32, (NZ * PADX, LANES), 0)
    return (row % PADX) * NZ + row // PADX


def spread_body(planes, feature_ref, cotangent_ref, index_ref, weight_ref, out_ref):
    cells = row_cells()
    channels = feature_ref.shape[0]

    def chunk(step, carry):
        parts = [[], []]
        for q in range(ROWS):
            lanes = pl.ds(pl.multiple_of((step * ROWS + q) * LANES, LANES), LANES)
            block = corner_block(index_ref, weight_ref, lanes, cells)
            stacked = jnp.concatenate([feature_ref[:, lanes], cotangent_ref[:, lanes]], axis=0)
            sums = contract(block, stacked, (1, 1))
            for f in range(2):
                parts[f].append(
                    jnp.concatenate(
                        [
                            sums[z * PADX : (z + 1) * PADX, f * channels : (f + 1) * channels]
                            for z in range(NZ)
                        ],
                        axis=1,
                    )
                )
        for f in range(2):
            turned = jnp.transpose(jnp.stack(parts[f]), (1, 0, 2))
            out_ref[f, :, pl.ds(pl.multiple_of(step * ROWS, ROWS), ROWS), :] = turned[:planes]
        return carry

    lax.fori_loop(0, out_ref.shape[2] // ROWS, chunk, 0)


def spread(features, cotangent, index, weight, planes, steps):
    channels, atoms = features.shape
    wide = atoms // steps
    by_lane = lambda i: (0, i)
    return pl.pallas_call(
        lambda *refs: spread_body(planes, *refs),
        grid=(steps,),
        out_shape=shape_of((2, planes, NY, LANES), F32),
        in_specs=[
            pl.BlockSpec((channels, wide), by_lane),
            pl.BlockSpec((channels, wide), by_lane),
            pl.BlockSpec((CORNERS, wide), by_lane),
            pl.BlockSpec((CORNERS, wide), by_lane),
        ],
        out_specs=pl.BlockSpec((2, planes, NY // steps, LANES), lambda i: (0, 0, i, 0)),
    )(features, cotangent, index, weight)


def gather_body(pulled_ref, index_ref, weight_ref, out_ref):
    cells = row_cells()
    channels = out_ref.shape[0]

    def chunk(step, carry):
        rows = pl.ds(pl.multiple_of(step * ROWS, ROWS), ROWS)
        turned = jnp.transpose(pulled_ref[:, rows, :], (1, 0, 2))
        for q in range(ROWS):
            lanes = pl.ds(pl.multiple_of((step * ROWS + q) * LANES, LANES), LANES)
            block = corner_block(index_ref, weight_ref, lanes, cells)
            plane = turned[q]
            tall = jnp.concatenate(
                [plane[:, z * channels : (z + 1) * channels] for z in range(NZ)], axis=0
            )
            out_ref[:, lanes] = contract(tall.astype(BF), block, (0, 0)).astype(BF)
        return carry

    lax.fori_loop(0, pulled_ref.shape[1] // ROWS, chunk, 0)


def gather(pulled, index, weight, channels, steps):
    atoms = index.shape[1]
    wide = atoms // steps
    by_lane = lambda i: (0, i)
    return pl.pallas_call(
        gather_body,
        grid=(steps,),
        out_shape=shape_of((channels, atoms), BF),
        in_specs=[
            pl.BlockSpec((PADX, NY // steps, LANES), lambda i: (0, i, 0)),
            pl.BlockSpec((CORNERS, wide), by_lane),
            pl.BlockSpec((CORNERS, wide), by_lane),
        ],
        out_specs=pl.BlockSpec((channels, wide), by_lane),
    )(pulled, index, weight)


def rim_body(count, planes, sums_ref, low_ref, high_ref, send_sem, recv_sem):
    me = lax.axis_index("brick")
    above = lax.rem(me + 1, count)
    below = lax.rem(me + count - 1, count)
    barrier = pltpu.get_barrier_semaphore()
    for other in (above, below):
        pl.semaphore_signal(barrier, inc=1, device_id={"brick": other}, device_id_type=MESH)
    pl.semaphore_wait(barrier, 2)
    copies = []
    top = planes - 2
    for slot, (src, dst, other) in enumerate(
        [
            (sums_ref.at[0, pl.ds(top, 2)], low_ref.at[pl.ds(0, 2)], above),
            (sums_ref.at[1, pl.ds(top + 1, 1)], low_ref.at[pl.ds(2, 1)], above),
            (sums_ref.at[0, pl.ds(0, 2)], high_ref.at[pl.ds(0, 2)], below),
            (sums_ref.at[1, pl.ds(0, 1)], high_ref.at[pl.ds(2, 1)], below),
        ]
    ):
        copy = pltpu.make_async_remote_copy(
            src_ref=src, dst_ref=dst, send_sem=send_sem.at[slot], recv_sem=recv_sem.at[slot],
            device_id={"brick": other}, device_id_type=MESH,
        )
        copy.start()
        copies.append(copy)
    for copy in copies:
        copy.wait()


def remote_call(body, out_shape, count, sems, collective, scratch=()):
    return pl.pallas_call(
        body,
        out_shape=out_shape,
        in_specs=[vmem()] * count,
        out_specs=jax.tree.map(lambda _: vmem(), out_shape),
        scratch_shapes=list(scratch)
        + [pltpu.SemaphoreType.DMA(sems), pltpu.SemaphoreType.DMA(sems)],
        compiler_params=pltpu.CompilerParams(collective_id=collective, has_side_effects=True),
    )


def mix_body(planes, sums_ref, low_ref, high_ref, taps_ref, order_ref, state_ref, grad_ref, mixed_ref, cat):
    wide = planes + 2
    order = order_ref[...]

    def send(field, out_ref, plane):
        turned = contract(order, field.astype(BF), (1, 1))
        out_ref[plane] = turned.reshape(out_ref.shape[1:]).astype(BF)

    for plane in range(wide):
        value = sums_ref[0, plane]
        if plane < 2:
            value = value + low_ref[plane]
        if plane >= wide - 2:
            value = value + high_ref[plane - (wide - 2)]
        rounded = value.astype(BF)
        state_ref[plane] = rounded
        value = rounded.astype(F32)
        cat[plane] = jnp.concatenate(
            [jnp.roll(value, 1, axis=0), value, jnp.roll(value, -1, axis=0)], axis=1
        ).astype(BF)
    for plane in range(planes):
        value = sums_ref[1, plane + 1]
        if plane == 0:
            value = value + low_ref[2]
        if plane == planes - 1:
            value = value + high_ref[2]
        send(value, grad_ref, plane)
    for plane in range(planes):
        total = state_ref[plane + 1].astype(F32)
        for dx in range(3):
            total = total + contract(cat[plane + dx], taps_ref[dx], (1, 0))
        send(total, mixed_ref, plane)


def greet(count, snaps):
    me = lax.axis_index("brick")
    side = lax.axis_index("snap")
    total = count * snaps
    flat = side * count + me
    barrier = pltpu.get_barrier_semaphore()

    def hello(step, carry):
        other = lax.rem(flat + step, total)
        pl.semaphore_signal(
            barrier, inc=1,
            device_id={"snap": other // count, "brick": lax.rem(other, count)},
            device_id_type=MESH,
        )
        return carry

    lax.fori_loop(1, total, hello, 0)
    pl.semaphore_wait(barrier, total - 1)
    return flat, total


def greet_bricks(count):
    me = lax.axis_index("brick")
    barrier = pltpu.get_barrier_semaphore()

    def hello(step, carry):
        pl.semaphore_signal(
            barrier, inc=1, device_id={"brick": lax.rem(me + step, count)}, device_id_type=MESH
        )
        return carry

    lax.fori_loop(1, count, hello, 0)
    pl.semaphore_wait(barrier, count - 1)
    return me


def run_all(total, make):
    def go(step, carry):
        for copy in make(step):
            copy.start()
        return carry

    def finish(step, carry):
        for copy in make(step):
            copy.wait()
        return carry

    lax.fori_loop(1, total, go, 0)
    return lambda: lax.fori_loop(1, total, finish, 0)


def forward_body(count, per, grad_ref, mixed_ref, gain_ref, grad_out, mixed_out, gain_out, send_sem, recv_sem):
    me = greet_bricks(count)
    planes = grad_ref.shape[0]

    def blocks(target):
        return [
            (grad_ref.at[:, target], grad_out.at[pl.ds(me * planes, planes)]),
            (mixed_ref.at[:, target], mixed_out.at[pl.ds(me * planes, planes)]),
            (gain_ref.at[pl.ds(target * per, per)], gain_out.at[:, me]),
        ]

    def make(step):
        target = lax.rem(me + step, count)
        return [
            pltpu.make_async_remote_copy(
                src_ref=src, dst_ref=dst, send_sem=send_sem.at[kind, step],
                recv_sem=recv_sem.at[kind, step], device_id={"brick": target},
                device_id_type=MESH,
            )
            for kind, (src, dst) in enumerate(blocks(target))
        ]

    finish = run_all(count, make)
    own = [
        pltpu.make_async_copy(src, dst, recv_sem.at[kind, 0])
        for kind, (src, dst) in enumerate(blocks(me))
    ]
    for copy in own:
        copy.start()
    for copy in own:
        copy.wait()
    finish()


def spectral_body(scale, back_scale, grad_ref, mixed_ref, gain_ref, rows_ref, cols_ref, inv_cols_ref, inv_rows_ref, ext_ref, part_ref, grad_f, mixed_f, back_f):
    length = grad_ref.shape[0]
    group = grad_ref.shape[1]
    per = gain_ref.shape[0]
    grad_f[...] = grad_ref[...].astype(F32)
    mixed_f[...] = mixed_ref[...].astype(F32)
    rows = rows_ref[...]
    cols = cols_ref[...]
    inv_cols = inv_cols_ref[...]
    inv_rows = inv_rows_ref[...]

    def transform(field):
        first = contract(field, rows, (1, 0), HIGHEST)
        tall = jnp.concatenate([first[:, :NY], first[:, NY:]], axis=0)
        return contract(cols, tall, (1, 0), HIGHEST)

    for channel in range(per):
        gain = jnp.transpose(gain_ref[channel].reshape(NY, length), (1, 0))
        gain = jnp.concatenate([gain, gain], axis=0)
        part = jnp.zeros((length, NY), F32)
        for z in range(NZ):
            p = z * per + channel
            spectrum = transform(grad_f[:, p, :])
            other = transform(mixed_f[:, p, :])
            product = spectrum * other
            part = part + product[:length] + product[length:]
            back = contract(inv_cols, spectrum * gain, (1, 0), HIGHEST)
            flat = jnp.concatenate([back[:length], back[length:]], axis=1)
            back_f[:, p, :] = contract(flat, inv_rows, (1, 0), HIGHEST) * back_scale
        part = jnp.transpose(part * scale, (1, 0))
        part_ref[channel] = part.reshape(part_ref.shape[1:])
    ext_ref[pl.ds(2, length)] = back_f[...].astype(BF)
    ext_ref[pl.ds(0, 2)] = back_f[pl.ds(length - 2, 2)].astype(BF)
    ext_ref[pl.ds(length + 2, 2)] = back_f[pl.ds(0, 2)].astype(BF)


def backward_body(count, snaps, planes, per, ext_ref, part_ref, ret_ref, gain_ref, send_sem, recv_sem):
    flat, total = greet(count, snaps)
    me = lax.rem(flat, count)
    side = flat // count

    def field(target):
        return (ext_ref.at[pl.ds(target * planes, planes + 4)], ret_ref.at[:, me])

    def gains(target):
        return (part_ref.at[:, target], gain_ref.at[side, pl.ds(me * per, per)])

    def make_field(step):
        target = lax.rem(me + step, count)
        src, dst = field(target)
        return [
            pltpu.make_async_remote_copy(
                src_ref=src, dst_ref=dst, send_sem=send_sem.at[0, step],
                recv_sem=recv_sem.at[0, step], device_id={"brick": target}, device_id_type=MESH,
            )
        ]

    def make_gain(step):
        other = lax.rem(flat + step, total)
        target = lax.rem(other, count)
        src, dst = gains(target)
        return [
            pltpu.make_async_remote_copy(
                src_ref=src, dst_ref=dst, send_sem=send_sem.at[1, step],
                recv_sem=recv_sem.at[1, step],
                device_id={"snap": other // count, "brick": target}, device_id_type=MESH,
            )
        ]

    finish_field = run_all(count, make_field)
    finish_gain = run_all(total, make_gain)
    own = [
        pltpu.make_async_copy(src, dst, recv_sem.at[kind, 0])
        for kind, (src, dst) in enumerate([field(me), gains(me)])
    ]
    for copy in own:
        copy.start()
    for copy in own:
        copy.wait()
    finish_field()
    finish_gain()


def pull_body(planes, channels, scale, ret_ref, state_ref, taps_ref, order_ref, pulled_ref, part_ref, cat):
    order = order_ref[...]
    for plane in range(planes + 4):
        field = ret_ref[plane].astype(F32).reshape(LANES, NY).astype(BF)
        value = contract(field, order, (0, 0))
        cat[plane] = jnp.concatenate(
            [jnp.roll(value, 1, axis=0), value, jnp.roll(value, -1, axis=0)], axis=1
        ).astype(BF)
    for plane in range(planes + 2):
        total = cat[plane + 1, :, LANES : 2 * LANES].astype(F32)
        for dx in range(3):
            total = total + contract(cat[plane + dx], taps_ref[dx], (1, 0))
        pulled_ref[plane] = total.astype(BF).astype(F32)
    for plane in range(planes + 2, PADX):
        pulled_ref[plane] = jnp.zeros((NY, LANES), F32)
    own = cat[pl.ds(2, planes)].reshape(planes * NY, 3 * LANES)
    lane = lax.broadcasted_iota(jnp.int32, (channels, LANES), 1) // channels
    groups = [jnp.zeros((channels, LANES), F32) for _ in range(part_ref.shape[0])]
    for dx in range(3):
        near = state_ref[pl.ds(dx, planes)].reshape(planes * NY, LANES)
        gram = contract(near, own, (0, 0))
        for dy in range(3):
            square = gram[:, (2 - dy) * LANES : (3 - dy) * LANES]
            for dz in range(3):
                line = jnp.zeros((channels, LANES), F32)
                for z in range(NZ):
                    source = z + dz - 1
                    if 0 <= source < NZ:
                        line = jnp.where(
                            lane == z, square[source * channels : (source + 1) * channels], line
                        )
                line = line + pltpu.roll(line, LANES // 2, 1)
                line = line + pltpu.roll(line, LANES // 4, 1)
                tap = 9 * dx + 3 * dy + dz
                groups[tap // NZ] = jnp.where(lane == tap % NZ, line * scale, groups[tap // NZ])
    for position, value in enumerate(groups):
        part_ref[position] = value


def reduce_body(count, snaps, part_ref, out_ref, landed, mine, send_sem, recv_sem):
    flat, total = greet(count, snaps)

    def where(step):
        other = lax.rem(flat + step, total)
        return other, {"snap": other // count, "brick": lax.rem(other, count)}

    def scatter(step):
        other, device = where(step)
        return [
            pltpu.make_async_remote_copy(
                src_ref=part_ref.at[other], dst_ref=landed.at[flat],
                send_sem=send_sem.at[0, step], recv_sem=recv_sem.at[0, step],
                device_id=device, device_id_type=MESH,
            )
        ]

    def spread_out(step):
        other, device = where(step)
        return [
            pltpu.make_async_remote_copy(
                src_ref=mine, dst_ref=out_ref.at[flat],
                send_sem=send_sem.at[1, step], recv_sem=recv_sem.at[1, step],
                device_id=device, device_id_type=MESH,
            )
        ]

    finish = run_all(total, scatter)
    own = pltpu.make_async_copy(part_ref.at[flat], landed.at[flat], recv_sem.at[0, 0])
    own.start()
    own.wait()
    finish()
    mine[...] = jnp.sum(landed[...], axis=0)
    finish = run_all(total, spread_out)
    own = pltpu.make_async_copy(mine, out_ref.at[flat], recv_sem.at[1, 0])
    own.start()
    own.wait()
    finish()


def banded(taps):
    channels = taps.shape[1]
    wide = jnp.tile(taps, (1, 1, NZ)).reshape(3, 3, 3, 1, channels, NZ * channels)
    level = jnp.arange(NZ)[:, None]
    column = jnp.arange(NZ * channels)[None, :] // channels
    total = jnp.zeros((), taps.dtype)
    for dz in range(3):
        fits = (column == level - (dz - 1))[None, None, :, None, :]
        total = total + jnp.where(fits, wide[:, :, dz], jnp.zeros((), taps.dtype))
    return total.reshape(3, 3 * NZ * channels, NZ * channels)


def fast_shards(sizes, atom_features, cotangent, cell_index, assign_weight, conv_kernel, spectral_gain):
    snaps, bricks = sizes
    channels = atom_features.shape[1]
    planes = NX // bricks
    per = channels // bricks
    group = NZ * per
    index = cell_index[0]
    weight = assign_weight[0]
    sums = spread(atom_features[0], cotangent[0], index, weight, planes + 2, 4)
    rim = shape_of((3, NY, LANES), F32)
    low, high = remote_call(
        lambda *refs: rim_body(bricks, planes + 2, *refs), [rim, rim], 1, (4,), 1
    )(sums)
    order = np.zeros((LANES, LANES), np.float32)
    for brick in range(bricks):
        for z in range(NZ):
            for c in range(per):
                order[brick * group + z * per + c, z * channels + brick * per + c] = 1.0
    order = jnp.asarray(order, BF)
    send = shape_of((planes, bricks, group, NY), BF)
    state, grad_send, mixed_send = local_call(
        lambda *refs: mix_body(planes, *refs),
        [shape_of((planes + 2, NY, LANES), BF), send, send], 5,
        [pltpu.VMEM((planes + 2, NY, 3 * LANES), BF)],
    )(sums, low, high, banded(conv_kernel), order)
    gain_turned = jnp.transpose(spectral_gain, (0, 2, 1))
    slab = shape_of((NX, group, NY), BF)
    grad_slab, mixed_slab, gain_slab = remote_call(
        lambda *refs: forward_body(bricks, per, *refs),
        [slab, slab, shape_of((per, bricks, NY // bricks, NX), F32)], 3, (3, bricks), 2,
    )(grad_send, mixed_send, gain_turned)

    def angles(length):
        phase = np.outer(np.arange(length), np.arange(length)) % length
        turn = 2.0 * np.pi * phase / length
        return np.cos(turn), np.sin(turn)

    col_cos, col_sin = angles(NX)
    row_cos, row_sin = angles(NY)
    rows = jnp.asarray(np.concatenate([row_cos, -row_sin], axis=1), F32)
    cols = jnp.asarray(np.block([[col_cos, col_sin], [-col_sin, col_cos]]), F32)
    inv_cols = jnp.asarray(np.block([[col_cos, -col_sin], [col_sin, col_cos]]), F32)
    inv_rows = jnp.asarray(np.concatenate([row_cos, -row_sin], axis=0), F32)
    scale = 1.0 / (NX * NY * math.sqrt(snaps * NZ))
    ext, part = local_call(
        lambda *refs: spectral_body(scale, 1.0 / (NX * NY), *refs),
        [shape_of((NX + 4, group, NY), BF), shape_of((per, bricks, NY // bricks, NX), F32)], 7,
        [pltpu.VMEM((NX, group, NY), F32)] * 3,
    )(grad_slab, mixed_slab, gain_slab, rows, cols, inv_cols, inv_rows)
    ret, gain_parts = remote_call(
        lambda *refs: backward_body(bricks, snaps, planes, per, *refs),
        [
            shape_of((planes + 4, bricks, group, NY), BF),
            shape_of((snaps, channels, NY // bricks, NX), F32),
        ],
        2, (2, bricks * snaps), 3,
    )(ext, part)
    gain_grad = jnp.transpose(jnp.sum(gain_parts, axis=0), (0, 2, 1))
    pulled, kernel_part = local_call(
        lambda *refs: pull_body(planes, channels, 1.0 / math.sqrt(snaps * NX * NY * NZ), *refs),
        [shape_of((PADX, NY, LANES), F32), shape_of((8, channels, LANES), F32)], 4,
        [pltpu.VMEM((planes + 4, NY, 3 * LANES), BF)],
    )(ret, state, banded(jnp.transpose(conv_kernel[::-1], (0, 2, 1))), order)
    total = bricks * snaps
    piece = 8 * channels // total
    summed = remote_call(
        lambda *refs: reduce_body(bricks, snaps, *refs),
        shape_of((total, piece, LANES), F32), 1, (2, total), 4,
        [pltpu.VMEM((total, piece, LANES), F32), pltpu.VMEM((piece, LANES), F32)],
    )(kernel_part.reshape(total, piece, LANES))
    kernel_grad = summed.reshape(8, channels, NZ, channels).transpose(0, 2, 1, 3)
    kernel_grad = kernel_grad.reshape(8 * NZ, channels, channels)[: conv_kernel.shape[0]]
    atom_grad = gather(pulled, index, weight, channels, 4)[None]
    return (atom_grad, kernel_grad, gain_grad)


def fits(mesh, channels, atoms):
    bricks = mesh.shape["brick"]
    snaps = mesh.shape["snap"]
    return (
        channels * NZ == LANES
        and NX == LANES
        and NY == LANES
        and atoms // bricks == NY * LANES
        and channels % bricks == 0
        and NZ * channels // bricks == ROWS
        and NX // bricks == ROWS
        and (8 * channels) % (bricks * snaps * ROWS) == 0
    )


def solution(mesh):
    placed = (
        P("snap", None, "brick"),
        P("snap", None, "brick"),
        P("snap", None, "brick"),
        P("snap", None, "brick"),
        P(),
        P(None, None, "brick"),
    )
    sizes = (mesh.shape["snap"], mesh.shape["brick"])

    def pick(*arguments):
        if fits(mesh, arguments[0].shape[1], arguments[0].shape[2] * sizes[1]):
            return fast_shards(sizes, *arguments)
        return shards(*arguments)

    return jax.shard_map(
        pick,
        mesh=mesh,
        in_specs=placed,
        out_specs=(P("snap", None, "brick"), P(), P(None, None, "brick")),
        check_vma=False,
    )
```

```python
import math

import jax
import jax.numpy as jnp
from jax import lax
import numpy as np
from jax.experimental import pallas as pl
from jax.experimental.pallas import tpu as pltpu
from jax.sharding import PartitionSpec as P

NX = 128
NY = 128
NZ = 4
CORNERS = 4


HIGHEST = lax.Precision.HIGHEST


def from_behind(value, axis, steps):
    count = lax.axis_size(axis)
    pairs = [(source, (source + steps) % count) for source in range(count)]
    return lax.ppermute(value, axis, pairs)


def with_halo(cells, sides, width):
    for axis, dim in sides:
        count = lax.axis_size(axis)
        head = lax.slice_in_dim(cells, 0, width, axis=dim)
        tail = lax.slice_in_dim(cells, cells.shape[dim] - width, cells.shape[dim], axis=dim)
        cells = jnp.concatenate(
            [
                lax.ppermute(tail, axis, [(i, (i + 1) % count) for i in range(count)]),
                cells,
                lax.ppermute(head, axis, [((i + 1) % count, i) for i in range(count)]),
            ],
            axis=dim,
        )
    return cells


def tables(length):
    indices = jnp.arange(length, dtype=jnp.int32)
    phases = indices[:, None] * indices[None, :] % length
    angles = phases.astype(jnp.float32) * (2.0 * math.pi / length)
    return (jnp.cos(angles), jnp.sin(angles))


def patches(padded, first_plane, planes):
    row_total = padded.shape[1]
    thickness = padded.shape[3]
    wrapped = jnp.concatenate([padded[:, -1:], padded, padded[:, :1]], axis=1)
    widened = jnp.pad(wrapped, ((0, 0), (0, 0), (0, 0), (1, 1)))
    pieces = []
    for step_first in (-1, 0, 1):
        for step_second in (-1, 0, 1):
            for step_third in (-1, 0, 1):
                pieces.append(
                    widened[
                        :,
                        1 + step_second : 1 + step_second + row_total,
                        first_plane + step_first : first_plane + step_first + planes,
                        1 + step_third : 1 + step_third + thickness,
                    ]
                )
    return jnp.stack(pieces)


def transform_rows(mesh_field, row_cosine, row_sine):
    real_part = jnp.einsum("cyxz,yk->ckxz", mesh_field, row_cosine, precision=HIGHEST)
    imag_part = -jnp.einsum("cyxz,yk->ckxz", mesh_field, row_sine, precision=HIGHEST)
    return jnp.stack([real_part, imag_part])


def transform_columns(stacked, col_cosine, col_sine, sign_value):

    def apply_table(part_values, table):
        return jnp.einsum("ckxz,xq->ckqz", part_values, table, precision=HIGHEST)

    real_part = stacked[0]
    imag_part = stacked[1]
    new_real = apply_table(real_part, col_cosine) + sign_value * apply_table(imag_part, col_sine)
    new_imag = apply_table(imag_part, col_cosine) - sign_value * apply_table(real_part, col_sine)
    return jnp.stack([new_real, new_imag])


def shards(atom_features, cotangent, cell_index, assign_weight, conv_kernel, spectral_gain):
    channels = atom_features.shape[1]
    slot_count = atom_features.shape[2] // NY
    own_planes = NX // lax.axis_size("brick")
    tile_cells = (own_planes + 2) * NZ
    snap_count = lax.axis_size("snap")
    index_tiles = cell_index[0].reshape(CORNERS, NY, slot_count)
    weight_tiles = assign_weight[0].astype(jnp.bfloat16).reshape(CORNERS, NY, slot_count)
    cell_numbers = jnp.arange(tile_cells, dtype=jnp.int32)
    blocks = jnp.zeros((NY, tile_cells, slot_count), jnp.bfloat16)
    for corner in range(CORNERS):
        matches = index_tiles[corner][:, None, :] == cell_numbers[None, :, None]
        blocks = blocks + jnp.where(
            matches, weight_tiles[corner][:, None, :], jnp.zeros((), jnp.bfloat16)
        )
    stacked = jnp.concatenate([atom_features[0], cotangent[0]], axis=0).reshape(
        2 * channels, NY, slot_count
    )
    spread = jnp.einsum("cts,tjs->ctj", stacked, blocks, preferred_element_type=jnp.float32)
    spread = spread.reshape(2 * channels, NY, own_planes + 2, NZ)
    from_above = from_behind(spread[:, :, 0], "brick", -1)
    from_below = from_behind(spread[:, :, own_planes + 1], "brick", 1)
    owned_planes = spread[:, :, 1 : own_planes + 1]
    owned_planes = owned_planes.at[:, :, 0].add(from_below)
    owned_planes = owned_planes.at[:, :, own_planes - 1].add(from_above)
    state_bf = owned_planes[:channels].astype(jnp.bfloat16)
    grad_mesh = owned_planes[channels:]
    col_cosine, col_sine = tables(NX)
    row_cosine, row_sine = tables(NY)

    def make_rows(mesh_field):
        return transform_rows(mesh_field, row_cosine, row_sine)

    def to_columns(part_rows):
        return transform_columns(part_rows, col_cosine, col_sine, 1.0)

    grad_rows = make_rows(grad_mesh)
    grad_spec = to_columns(
        lax.all_to_all(grad_rows, "brick", split_axis=2, concat_axis=3, tiled=True)
    )
    state_rim = with_halo(state_bf, (("brick", 2),), 1)
    state_patch = patches(state_rim, 1, own_planes)
    conv_out = jnp.einsum(
        "tcyxz,tcd->dyxz", state_patch, conv_kernel, preferred_element_type=jnp.float32
    )
    mesh_mixed = state_bf.astype(jnp.float32) + conv_out
    mixed_rows = make_rows(mesh_mixed)
    state_spec = to_columns(
        lax.all_to_all(
            mixed_rows.astype(jnp.bfloat16), "brick", split_axis=2, concat_axis=3, tiled=True
        ).astype(mixed_rows.dtype)
    )
    products = jnp.sum(grad_spec[0] * state_spec[0] + grad_spec[1] * state_spec[1], axis=3)
    gain_part = jnp.transpose(products, (0, 2, 1)) / (NX * NY * math.sqrt(snap_count * NZ))
    gain_local = jnp.transpose(spectral_gain, (0, 2, 1))
    filtered = grad_spec * gain_local[None, :, :, :, None]
    before_cross = transform_columns(filtered, col_cosine, col_sine, -1.0)
    part_cols = lax.all_to_all(before_cross, "brick", split_axis=3, concat_axis=2, tiled=True)
    real_rows = jnp.einsum("ckxz,ky->cyxz", part_cols[0], row_cosine, precision=HIGHEST)
    imag_rows = jnp.einsum("ckxz,ky->cyxz", part_cols[1], row_sine, precision=HIGHEST)
    grad_mixed = (real_rows - imag_rows) / (NX * NY)
    grad_bf = grad_mixed.astype(jnp.bfloat16)
    flipped = conv_kernel[::-1]
    grad_padded = with_halo(grad_bf, (("brick", 2),), 1)
    grad_patch = patches(grad_padded, 1, own_planes)
    back_conv = jnp.einsum(
        "tdyxz,tcd->cyxz", grad_patch, flipped, preferred_element_type=jnp.float32
    )
    pulled = (grad_bf.astype(jnp.float32) + back_conv).astype(jnp.bfloat16)
    pulled_full = with_halo(pulled, (("brick", 2),), 1)
    kernel_part = jnp.einsum(
        "tcyxz,dyxz->tcd", state_patch, grad_bf, preferred_element_type=jnp.float32
    )
    kernel_part = kernel_part / math.sqrt(snap_count * NX * NY * NZ)
    pulled_tiles = pulled_full.reshape(channels, NY, tile_cells)
    atom_total = jnp.einsum(
        "ctj,tjs->cts", pulled_tiles, blocks, preferred_element_type=jnp.float32
    )
    atom_grad = atom_total.astype(jnp.bfloat16).reshape(1, channels, NY * slot_count)
    kernel_grad = lax.psum(kernel_part, ("snap", "brick"))
    gain_grad = lax.psum(gain_part, "snap")
    return (atom_grad, kernel_grad, gain_grad)


BF = jnp.bfloat16
F32 = jnp.float32
LANES = 128
ROWS = 8
PADX = 16
MESH = pl.DeviceIdType.MESH


def contract(left, right, dims, precision=None):
    return lax.dot_general(
        left, right, ((dims[:1], dims[1:]), ((), ())),
        precision=precision, preferred_element_type=F32,
    )


def vmem():
    return pl.BlockSpec(memory_space=pltpu.VMEM)


def shape_of(dims, kind):
    return jax.ShapeDtypeStruct(dims, kind)


def corner_block(index_ref, weight_ref, lanes, cell_of_row):
    block = jnp.zeros(cell_of_row.shape, F32)
    index = index_ref[:, lanes]
    weight = weight_ref[:, lanes]
    for corner in range(CORNERS):
        block = jnp.where(
            index[corner : corner + 1] == cell_of_row, weight[corner : corner + 1], block
        )
    return block.astype(BF)


def row_cells():
    row = lax.broadcasted_iota(jnp.int32, (NZ * PADX, LANES), 0)
    return (row % PADX) * NZ + row // PADX


def run_all(first, total, make):
    def go(step, carry):
        make(step).start()
        return carry

    lax.fori_loop(first, total, go, 0)


def wait_all(first, total, make):
    def finish(step, carry):
        make(step).wait()
        return carry

    lax.fori_loop(first, total, finish, 0)


def split(value):
    high = value.astype(BF)
    return high, (value - high.astype(F32)).astype(BF)


def three(left, right):
    left_high, left_low = left
    right_high, right_low = right
    return (
        contract(left_high, right_high, (1, 0))
        + contract(left_high, right_low, (1, 0))
        + contract(left_low, right_high, (1, 0))
    )


def widen(value):
    return jnp.concatenate(
        [jnp.roll(value, 1, axis=0), value, jnp.roll(value, -1, axis=0)], axis=1
    ).astype(BF)


def whole_body(
    bricks, snaps, chunks,
    feature_ref, cotangent_ref, index_ref, weight_ref, taps_ref, gain_ref,
    order_ref, rows_ref, cols_ref, inv_cols_ref, inv_rows_ref,
    atom_ref, kernel_ref, gain_out_ref,
    blocks, sums, edge, low, high, band, back_band, state, cat, grad_send, mixed_send,
    grad_slab, mixed_slab, gain_slab, field_f, back_f, spectra, ext, ret, back_cat, pulled,
    gain_send, gain_land, kernel_part, kernel_land, kernel_mine, kernel_all,
    edge_send, edge_recv, out_send, out_recv, ret_send, ret_recv,
    gain_ssem, gain_rsem, red_send, red_recv, own_sem,
):
    channels = feature_ref.shape[0]
    planes = NX // bricks
    per = channels // bricks
    total = bricks * snaps
    me = lax.axis_index("brick")
    side = lax.axis_index("snap")
    flat = side * bricks + me
    above = lax.rem(me + 1, bricks)
    below = lax.rem(me + bricks - 1, bricks)
    barrier = pltpu.get_barrier_semaphore()

    def device_of(step):
        other = lax.rem(flat + step, total)
        return other, {"snap": other // bricks, "brick": lax.rem(other, bricks)}

    def hello(step, carry):
        pl.semaphore_signal(barrier, inc=1, device_id=device_of(step)[1], device_id_type=MESH)
        return carry

    lax.fori_loop(1, total, hello, 0)

    def remote(src, dst, send_sem, recv_sem, device):
        return pltpu.make_async_remote_copy(
            src_ref=src, dst_ref=dst, send_sem=send_sem, recv_sem=recv_sem,
            device_id=device, device_id_type=MESH,
        )

    def local(src, dst):
        copy = pltpu.make_async_copy(src, dst, own_sem)
        copy.start()
        copy.wait()

    cells = row_cells()

    def spread_step(step, carry):
        parts = [[], []]
        for q in range(ROWS):
            y = step * ROWS + q
            lanes = pl.ds(pl.multiple_of(y * LANES, LANES), LANES)
            block = corner_block(index_ref, weight_ref, lanes, cells)
            blocks[y] = block
            stacked = jnp.concatenate([feature_ref[:, lanes], cotangent_ref[:, lanes]], axis=0)
            found = contract(block, stacked, (1, 1))
            for f in range(2):
                parts[f].append(
                    jnp.concatenate(
                        [
                            found[z * PADX : (z + 1) * PADX, f * channels : (f + 1) * channels]
                            for z in range(NZ)
                        ],
                        axis=1,
                    )
                )
        for f in range(2):
            turned = jnp.transpose(jnp.stack(parts[f]), (1, 0, 2))
            sums[f, :, pl.ds(pl.multiple_of(step * ROWS, ROWS), ROWS), :] = turned[: planes + 2]
        return carry

    def gain_copy(step):
        target = lax.rem(me + step, bricks)
        return remote(
            gain_ref.at[pl.ds(target * per, per)], gain_slab.at[:, me],
            out_send.at[2, step], out_recv.at[2, step], {"brick": target},
        )

    def edge_copy(chunk, way):
        rows = pl.ds(chunk * (NY // chunks), NY // chunks)
        land = low if way == 0 else high
        return remote(
            edge.at[pl.ds(3 * way, 3), rows], land.at[:, rows],
            edge_send.at[way, chunk], edge_recv.at[way, chunk],
            {"brick": above if way == 0 else below},
        )

    span = NY // chunks
    for chunk in range(chunks):
        lax.fori_loop(chunk * (span // ROWS), (chunk + 1) * (span // ROWS), spread_step, 0)
        rows = pl.ds(chunk * span, span)
        for slot, (f, plane) in enumerate(
            [(0, planes), (0, planes + 1), (1, planes + 1), (0, 0), (0, 1), (1, 0)]
        ):
            edge[slot, rows, :] = sums[f, plane, rows, :].astype(BF)
        if chunk == 0:
            pl.semaphore_wait(barrier, total - 1)
        for way in range(2):
            edge_copy(chunk, way).start()
    run_all(1, bricks, gain_copy)
    local(gain_ref.at[pl.ds(me * per, per)], gain_slab.at[:, me])

    lane = lax.broadcasted_iota(jnp.int32, (channels, LANES), 1) // channels
    for dx in range(3):
        for dy in range(3):
            tiled = []
            for dz in range(3):
                tap = taps_ref[9 * dx + 3 * dy + dz].astype(F32)
                tiled.append(jnp.concatenate([tap] * NZ, axis=1))
            lines = []
            for z in range(NZ):
                line = jnp.zeros((channels, LANES), F32)
                for dz in range(3):
                    line = jnp.where(lane == z - (dz - 1), tiled[dz], line)
                lines.append(line)
            square = jnp.concatenate(lines, axis=0)
            band[dx, dy * LANES : (dy + 1) * LANES, :] = square.astype(BF)
            back_band[2 - dx, (2 - dy) * LANES : (3 - dy) * LANES, :] = jnp.transpose(
                square, (1, 0)
            ).astype(BF)

    order = order_ref[...]

    def place(field, out, plane):
        turned = contract(order, field.astype(BF), (1, 1))
        out[plane] = turned.reshape(out.shape[1:]).astype(BF)

    def field_copy(kind, send, slab):
        def make(step):
            target = lax.rem(me + step, bricks)
            return remote(
                send.at[:, target], slab.at[pl.ds(me * planes, planes)],
                out_send.at[kind, step], out_recv.at[kind, step], {"brick": target},
            )

        return make

    grad_copy = field_copy(0, grad_send, grad_slab)
    mixed_copy = field_copy(1, mixed_send, mixed_slab)

    for plane in range(1, planes - 1):
        place(sums[1, plane + 1], grad_send, plane)
    for chunk in range(chunks):
        for way in range(2):
            edge_copy(chunk, way).wait()
    place(sums[1, 1] + low[2].astype(F32), grad_send, 0)
    place(sums[1, planes] + high[2].astype(F32), grad_send, planes - 1)
    run_all(1, bricks, grad_copy)
    local(grad_send.at[:, me], grad_slab.at[pl.ds(me * planes, planes)])

    for plane in range(planes + 2):
        value = sums[0, plane]
        if plane < 2:
            value = value + low[plane].astype(F32)
        if plane >= planes:
            value = value + high[plane - planes].astype(F32)
        rounded = value.astype(BF)
        state[plane] = rounded
        cat[plane] = widen(rounded.astype(F32))
    for plane in range(planes):
        value = state[plane + 1].astype(F32)
        for dx in range(3):
            value = value + contract(cat[plane + dx], band[dx], (1, 0))
        place(value, mixed_send, plane)
    run_all(1, bricks, mixed_copy)
    local(mixed_send.at[:, me], mixed_slab.at[pl.ds(me * planes, planes)])

    rows = rows_ref[...]
    cols = (cols_ref[0], cols_ref[1])
    inv_cols = (inv_cols_ref[0], inv_cols_ref[1])
    inv_rows = (inv_rows_ref[0], inv_rows_ref[1])

    def transform(channel):
        tall = jnp.concatenate([field_f[:, z * per + channel, :] for z in range(NZ)], axis=0)
        tall = tall.astype(BF)
        first = contract(jnp.concatenate([tall, tall], axis=1), rows, (1, 0))
        halves = []
        for half in range(2):
            halves.append(
                jnp.concatenate(
                    [
                        first[z * NX : (z + 1) * NX, half * NY : (half + 1) * NY]
                        for z in range(NZ)
                    ],
                    axis=1,
                )
            )
        return three(cols, split(jnp.concatenate(halves, axis=0)))

    wait_all(1, bricks, grad_copy)
    wait_all(1, bricks, gain_copy)
    field_f[...] = grad_slab[...].astype(F32)
    for channel in range(per):
        spectra[channel] = transform(channel)
        gain = jnp.transpose(gain_slab[channel].reshape(NY, NX), (1, 0))
        gain = jnp.concatenate([gain] * NZ, axis=1)
        gain = jnp.concatenate([gain, gain], axis=0)
        back = three(inv_cols, split(spectra[channel] * gain))
        flats = []
        for z in range(NZ):
            piece = back[:, z * NY : (z + 1) * NY]
            flats.append(jnp.concatenate([piece[:NX], piece[NX:]], axis=1))
        out = three(split(jnp.concatenate(flats, axis=0)), inv_rows) * (1.0 / (NX * NY))
        for z in range(NZ):
            back_f[:, z * per + channel, :] = out[z * NX : (z + 1) * NX]
    ext[pl.ds(2, NX)] = back_f[...].astype(BF)
    ext[pl.ds(0, 2)] = back_f[pl.ds(NX - 2, 2)].astype(BF)
    ext[pl.ds(NX + 2, 2)] = back_f[pl.ds(0, 2)].astype(BF)

    def ret_copy(step):
        target = lax.rem(me + step, bricks)
        return remote(
            ext.at[pl.ds(target * planes, planes + 4)], ret.at[:, me],
            ret_send.at[step], ret_recv.at[step], {"brick": target},
        )

    run_all(1, bricks, ret_copy)
    local(ext.at[pl.ds(me * planes, planes + 4)], ret.at[:, me])

    wait_all(1, bricks, mixed_copy)
    field_f[...] = mixed_slab[...].astype(F32)
    scale = 1.0 / (NX * NY * math.sqrt(snaps * NZ))
    for channel in range(per):
        product = spectra[channel] * transform(channel)
        product = product[:NX] + product[NX:]
        part = product[:, :NY]
        for z in range(1, NZ):
            part = part + product[:, z * NY : (z + 1) * NY]
        part = jnp.transpose(part * scale, (1, 0))
        gain_send[channel] = part.reshape(gain_send.shape[1:]).astype(gain_send.dtype)

    def part_copy(step):
        other, device = device_of(step)
        return remote(
            gain_send.at[:, lax.rem(other, bricks)], gain_land.at[side, pl.ds(me * per, per)],
            gain_ssem.at[step], gain_rsem.at[step], device,
        )

    wait_all(1, bricks, ret_copy)
    run_all(1, total, part_copy)
    local(gain_send.at[:, me], gain_land.at[side, pl.ds(me * per, per)])

    for plane in range(planes + 4):
        field = ret[plane].astype(F32).reshape(LANES, NY).astype(BF)
        back_cat[plane] = widen(contract(field, order, (0, 0)))
    own = back_cat[pl.ds(2, planes)].reshape(planes * NY, 3 * LANES)
    groups = [jnp.zeros((channels, LANES), F32) for _ in range(kernel_all.shape[0] * ROWS // channels)]
    tap_scale = 1.0 / math.sqrt(snaps * NX * NY * NZ)
    for dx in range(3):
        near = state[pl.ds(dx, planes)].reshape(planes * NY, LANES)
        gram = contract(near, own, (0, 0))
        for dy in range(3):
            square = gram[:, (2 - dy) * LANES : (3 - dy) * LANES]
            for dz in range(3):
                line = jnp.zeros((channels, LANES), F32)
                for z in range(NZ):
                    source = z + dz - 1
                    if 0 <= source < NZ:
                        line = jnp.where(
                            lane == z, square[source * channels : (source + 1) * channels], line
                        )
                line = line + pltpu.roll(line, LANES // 2, 1)
                line = line + pltpu.roll(line, LANES // 4, 1)
                tap = 9 * dx + 3 * dy + dz
                groups[tap // NZ] = jnp.where(
                    lane == tap % NZ, line * tap_scale, groups[tap // NZ]
                )
    tiles = channels // ROWS
    for position, value in enumerate(groups):
        kernel_part[position * tiles : (position + 1) * tiles] = value.reshape(tiles, ROWS, LANES)

    def scatter(step):
        other, device = device_of(step)
        return remote(
            kernel_part.at[other], kernel_land.at[flat],
            red_send.at[0, step], red_recv.at[0, step], device,
        )

    def share(step):
        _, device = device_of(step)
        return remote(
            kernel_mine, kernel_all.at[flat],
            red_send.at[1, step], red_recv.at[1, step], device,
        )

    run_all(1, total, scatter)
    local(kernel_part.at[flat], kernel_land.at[flat])

    for plane in range(planes + 2):
        value = back_cat[plane + 1, :, LANES : 2 * LANES].astype(F32)
        for dx in range(3):
            value = value + contract(back_cat[plane + dx], back_band[dx], (1, 0))
        pulled[plane] = value.astype(BF).astype(F32)
    for plane in range(planes + 2, PADX):
        pulled[plane] = jnp.zeros((NY, LANES), F32)

    wait_all(1, total, scatter)
    kernel_mine[...] = jnp.sum(kernel_land[...], axis=0)
    run_all(1, total, share)
    local(kernel_mine, kernel_all.at[flat])

    def gather_step(step, carry):
        here = pl.ds(pl.multiple_of(step * ROWS, ROWS), ROWS)
        turned = jnp.transpose(pulled[:, here, :], (1, 0, 2))
        for q in range(ROWS):
            y = step * ROWS + q
            lanes = pl.ds(pl.multiple_of(y * LANES, LANES), LANES)
            plane = turned[q]
            tall = jnp.concatenate(
                [plane[:, z * channels : (z + 1) * channels] for z in range(NZ)], axis=0
            )
            atom_ref[:, lanes] = contract(tall.astype(BF), blocks[y], (0, 0)).astype(BF)
        return carry

    lax.fori_loop(0, NY // ROWS, gather_step, 0)

    wait_all(1, total, part_copy)
    gain_sum = gain_land[0].astype(F32)
    for other in range(1, snaps):
        gain_sum = gain_sum + gain_land[other].astype(F32)
    gain_out_ref[...] = gain_sum
    wait_all(1, total, share)
    final = kernel_all[...].reshape(kernel_all.shape[0] * ROWS // channels, channels, LANES)
    for tap in range(kernel_ref.shape[0]):
        at = (tap % NZ) * channels
        kernel_ref[tap] = final[tap // NZ][:, at : at + channels]


def fast_shards(sizes, atom_features, cotangent, cell_index, assign_weight, conv_kernel, spectral_gain):
    snaps, bricks = sizes
    channels, atoms = atom_features.shape[1:]
    planes = NX // bricks
    per = channels // bricks
    group = NZ * per
    total = bricks * snaps
    chunks = 4
    order = np.zeros((LANES, LANES), np.float32)
    for brick in range(bricks):
        for z in range(NZ):
            for c in range(per):
                order[brick * group + z * per + c, z * channels + brick * per + c] = 1.0

    def angles(length):
        phase = np.outer(np.arange(length), np.arange(length)) % length
        turn = 2.0 * np.pi * phase / length
        return np.cos(turn), np.sin(turn)

    def halves(table):
        table = np.asarray(table, np.float32)
        high = table.astype(BF)
        low = (table - high.astype(np.float32)).astype(BF)
        return high, low

    col_cos, col_sin = angles(NX)
    row_cos, row_sin = angles(NY)
    rows = jnp.asarray(np.concatenate(halves(np.concatenate([row_cos, -row_sin], axis=1)), axis=0))
    cols = jnp.asarray(np.stack(halves(np.block([[col_cos, col_sin], [-col_sin, col_cos]]))))
    inv_cols = jnp.asarray(np.stack(halves(np.block([[col_cos, -col_sin], [col_sin, col_cos]]))))
    inv_rows = jnp.asarray(np.stack(halves(np.concatenate([row_cos, -row_sin], axis=0))))
    mesh_plane = (NY, LANES)
    send = (planes, bricks, group, NY)
    slab = (NX, group, NY)
    piece = (bricks, NY // bricks, NX)
    scratch = [
        ((NY, NZ * PADX, LANES), BF),
        ((2, planes + 2) + mesh_plane, F32),
        ((6,) + mesh_plane, BF),
        ((3,) + mesh_plane, BF),
        ((3,) + mesh_plane, BF),
        ((3, 3 * LANES, LANES), BF),
        ((3, 3 * LANES, LANES), BF),
        ((planes + 2,) + mesh_plane, BF),
        ((planes + 2, NY, 3 * LANES), BF),
        (send, BF),
        (send, BF),
        (slab, BF),
        (slab, BF),
        ((per,) + piece, F32),
        (slab, F32),
        (slab, F32),
        ((per, 2 * NX, NZ * NY), F32),
        ((NX + 4, group, NY), BF),
        ((planes + 4, bricks, group, NY), BF),
        ((planes + 4, NY, 3 * LANES), BF),
        ((PADX,) + mesh_plane, F32),
        ((per,) + piece, BF),
        ((snaps, channels) + piece[1:], BF),
        ((total, ROWS, LANES), F32),
        ((total, ROWS, LANES), F32),
        ((ROWS, LANES), F32),
        ((total, ROWS, LANES), F32),
    ]
    sems = [(2, chunks)] * 2 + [(3, bricks)] * 2 + [(bricks,)] * 2 + [(total,)] * 2 + [(2, total)] * 2
    atom_grad, kernel_grad, gain_grad = pl.pallas_call(
        lambda *refs: whole_body(bricks, snaps, chunks, *refs),
        out_shape=[
            shape_of((channels, atoms), BF),
            shape_of(conv_kernel.shape, F32),
            shape_of((channels,) + piece[1:], F32),
        ],
        in_specs=[vmem()] * 11,
        out_specs=[vmem()] * 3,
        scratch_shapes=[pltpu.VMEM(dims, kind) for dims, kind in scratch]
        + [pltpu.SemaphoreType.DMA(dims) for dims in sems]
        + [pltpu.SemaphoreType.DMA],
        compiler_params=pltpu.CompilerParams(
            collective_id=1, has_side_effects=True, vmem_limit_bytes=60 * 1024 * 1024
        ),
    )(
        atom_features[0], cotangent[0], cell_index[0], assign_weight[0], conv_kernel,
        jnp.transpose(spectral_gain, (0, 2, 1)), jnp.asarray(order, BF), rows, cols,
        inv_cols, inv_rows,
    )
    return (atom_grad[None], kernel_grad, jnp.transpose(gain_grad, (0, 2, 1)))


def fits(mesh, channels, atoms):
    bricks = mesh.shape["brick"]
    snaps = mesh.shape["snap"]
    return (
        channels * NZ == LANES
        and NX == LANES
        and NY == LANES
        and atoms // bricks == NY * LANES
        and channels % bricks == 0
        and NZ * channels // bricks == ROWS
        and NX // bricks == ROWS
        and 8 * channels == bricks * snaps * ROWS
    )


def solution(mesh):
    placed = (
        P("snap", None, "brick"),
        P("snap", None, "brick"),
        P("snap", None, "brick"),
        P("snap", None, "brick"),
        P(),
        P(None, None, "brick"),
    )
    sizes = (mesh.shape["snap"], mesh.shape["brick"])

    def pick(*arguments):
        if fits(mesh, arguments[0].shape[1], arguments[0].shape[2] * sizes[1]):
            return fast_shards(sizes, *arguments)
        return shards(*arguments)

    return jax.shard_map(
        pick,
        mesh=mesh,
        in_specs=placed,
        out_specs=(P("snap", None, "brick"), P(), P(None, None, "brick")),
        check_vma=False,
    )
```
